32 devices in a mesh: batch: 8 (over y, x, core), rows: 4 (over z).
Axes of the slice: x: 2, y: 2, z: 4, core: 2. Of those that a mesh axis runs over, the one named last changes fastest.
Arguments:
- fine_level: bfloat16 [8, 32, 192, 384], P('batch', 'rows'), may hold values from -40 to 40
- middle_level: bfloat16 [8, 16, 96, 384], P('batch', 'rows'), may hold values from -40 to 40
- coarse_level: bfloat16 [8, 8, 48, 384], P('batch', 'rows'), may hold values from -40 to 40
- two_input_weights: float32 [2, 3, 2], replicated, may hold values from 0.5 to 2
- three_input_weights: float32 [2, 3], replicated, may hold values from 0.5 to 2
- depthwise: bfloat16 [2, 4, 3, 3, 384], replicated, may hold values from -2 to 2
- pointwise: bfloat16 [2, 4, 384, 384], replicated, may hold values from -0.3125 to 0.3125
- bn_gain: float32 [2, 4, 384], replicated, may hold values from 0.5 to 1.5
- bn_bias: float32 [2, 4, 384], replicated, may hold values from -3 to 3
Outputs:
- fine_result: bfloat16 [8, 32, 192, 384], P('batch', 'rows')
- middle_result: bfloat16 [8, 16, 96, 384], P('batch', 'rows')
- coarse_result: bfloat16 [8, 8, 48, 384], P('batch', 'rows')
The draws below stay inside these ranges and needn't reach their ends.
All inputs are finite; a program needn't handle non-finite values.
Results may differ from the reference program's by a relative error of at most 0.025.
Values may be sent and summed in bfloat16 or wider, within the bound.
A program may use at most 64 MiB of HBM per device.

```python
import math
import jax
import jax.numpy as jnp
from jax import lax

C = 384
LAYERS = 2
COLS = 192
COLS_MID = 96
COLS_TOP = 48
HEIGHT = 32
HEIGHT_MID = 16
HEIGHT_TOP = 8
IMAGES = 8


def level_draw(key, height, width):
    noise_key = jax.random.fold_in(key, 11)
    channel_key = jax.random.fold_in(key, 12)
    offset_key = jax.random.fold_in(key, 13)
    shape = (IMAGES, height, width, C)
    noise = jnp.clip(jax.random.normal(noise_key, shape, jnp.float32), -4.0, 4.0)
    rise = math.log(3.0)
    channel_scale = jnp.exp(jax.random.uniform(channel_key, (C,), jnp.float32, math.log(0.3), math.log(3.0)))
    image_pos = jnp.arange(IMAGES, dtype=jnp.float32) / max(IMAGES - 1, 1)
    row_pos = jnp.arange(height, dtype=jnp.float32) / max(height - 1, 1)
    spatial_scale = jnp.exp(rise * (image_pos[:, None] + row_pos[None, :] - 1.0))
    offsets = 0.5 * jax.random.normal(offset_key, (IMAGES, 1, 1, C), jnp.float32)
    values = noise * spatial_scale[:, :, None, None] * channel_scale + offsets
    return jnp.clip(values, -40.0, 40.0).astype(jnp.bfloat16)


def draw_fine_level(key, part):
    return level_draw(key, HEIGHT, COLS)


def draw_middle_level(key, part):
    return level_draw(key, HEIGHT_MID, COLS_MID)


def draw_coarse_level(key, part):
    return level_draw(key, HEIGHT_TOP, COLS_TOP)


def gaussian(key, extent, scale, most, kind=jnp.bfloat16):
    entries = jax.random.normal(key, extent, jnp.float32) * scale
    return jnp.minimum(jnp.maximum(entries, -most), most).astype(kind)


def setup_inputs(seed: int = 0) -> dict:
    keys = jax.random.split(jax.random.key(seed), 10)
    return {
        "fine_level": draw_fine_level(jax.random.fold_in(keys[9], 71), 0),
        "middle_level": draw_middle_level(jax.random.fold_in(keys[9], 71), 0),
        "coarse_level": draw_coarse_level(jax.random.fold_in(keys[9], 71), 0),
        "two_input_weights": jnp.clip(jnp.exp(jax.random.uniform(keys[3], (LAYERS, 3, 2), jnp.float32, math.log(0.5), math.log(2.0))), 0.5, 2.0),
        "three_input_weights": jnp.clip(jnp.exp(jax.random.uniform(keys[4], (LAYERS, 3), jnp.float32, math.log(0.5), math.log(2.0))), 0.5, 2.0),
        "depthwise": gaussian(keys[5], (LAYERS, 4, 3, 3, C), 9 ** -0.5, 2.0),
        "pointwise": gaussian(keys[6], (LAYERS, 4, C, C), C ** -0.5, 0.3125),
        "bn_gain": jnp.clip(1.0 + 0.1 * jax.random.normal(keys[7], (LAYERS, 4, C), jnp.float32), 0.5, 1.5),
        "bn_bias": gaussian(keys[8], (LAYERS, 4, C), 0.5, 3.0, jnp.float32),
    }


def upsample(feature_maps):
    return jnp.repeat(jnp.repeat(feature_maps, 2, axis=1), 2, axis=2)

def reduce_resolution(feature_maps):
    lowest = jnp.array(-jnp.inf, feature_maps.dtype)
    padded = jnp.pad(feature_maps, ((0, 0), (0, 1), (0, 1), (0, 0)), constant_values=lowest)
    return lax.reduce_window(padded, lowest, lax.max, (1, 3, 3, 1), (1, 2, 2, 1), 'VALID')

def weighted_join_activate(inputs_list, weights):
    weight_sum = jnp.sum(weights) + 0.0001
    running = weights[0] * inputs_list[0].astype(jnp.float32)
    for position in range(1, len(inputs_list)):
        running = running + weights[position] * inputs_list[position].astype(jnp.float32)
    return jax.nn.silu(running / weight_sum).astype(jnp.bfloat16)

def separable(extended, kernel, projection):
    padded = jnp.pad(extended, ((0, 0), (0, 0), (1, 1), (0, 0)))
    height = extended.shape[1] - 2
    width = extended.shape[2]
    running = jnp.zeros((extended.shape[0], height, width, extended.shape[3]), jnp.float32)
    for row_tap in range(3):
        for col_tap in range(3):
            window = padded[:, row_tap:row_tap + height, col_tap:col_tap + width, :]
            running = running + window.astype(jnp.float32) * kernel[row_tap, col_tap].astype(jnp.float32)
    spatial = running.astype(jnp.bfloat16)
    projected = jnp.dot(spatial.reshape(-1, spatial.shape[-1]), projection, preferred_element_type=jnp.float32)
    return projected.reshape(spatial.shape)

def normalize(projected, gain, offset):
    center = lax.optimization_barrier(jnp.mean(projected, axis=(0, 1, 2)))
    centered = projected - center
    spread = lax.optimization_barrier(jnp.mean(centered * centered, axis=(0, 1, 2)))
    return (centered * lax.rsqrt(spread + 1e-05) * gain + offset).astype(jnp.bfloat16)

def node(activated, kernel, projection, gain, offset):
    padded = jnp.pad(activated, ((0, 0), (1, 1), (0, 0), (0, 0)))

    def one_image(image):
        return separable(image[None], kernel, projection)[0]
    projected = lax.map(one_image, padded)
    return normalize(projected, gain, offset)

def reference(fine_level, middle_level, coarse_level, two_input_weights, three_input_weights, depthwise, pointwise, bn_gain, bn_bias):
    fine, middle_grid, coarse_grid = (fine_level, middle_level, coarse_level)
    for bidirectional_layer in range(LAYERS):

        def run_layer_pair(index, activated):
            return node(activated, depthwise[bidirectional_layer, index], pointwise[bidirectional_layer, index], bn_gain[bidirectional_layer, index], bn_bias[bidirectional_layer, index])
        downward_middle = run_layer_pair(0, weighted_join_activate([middle_grid, upsample(coarse_grid)], two_input_weights[bidirectional_layer, 0]))
        updated_fine = run_layer_pair(1, weighted_join_activate([fine, upsample(downward_middle)], two_input_weights[bidirectional_layer, 1]))
        updated_middle = run_layer_pair(2, weighted_join_activate([middle_grid, downward_middle, reduce_resolution(updated_fine)], three_input_weights[bidirectional_layer]))
        updated_coarse = run_layer_pair(3, weighted_join_activate([coarse_grid, reduce_resolution(updated_middle)], two_input_weights[bidirectional_layer, 2]))
        fine, middle_grid, coarse_grid = (updated_fine, updated_middle, updated_coarse)
    return (fine, middle_grid, coarse_grid)
```

```python
import functools

import jax
import jax.numpy as jnp
from jax import lax
from jax.experimental import pallas as pl
from jax.experimental.pallas import tpu as pltpu
from jax.sharding import PartitionSpec as P

LAYERS = 2
NODES = 4
MESH = pl.DeviceIdType.MESH
F32 = jnp.float32
BF16 = jnp.bfloat16
PAD = 8


def permutation(size, phases, inverse):
    part = size // phases
    natural = lax.broadcasted_iota(jnp.int32, (size, size), 0 if inverse else 1)
    ordered = lax.broadcasted_iota(jnp.int32, (size, size), 1 if inverse else 0)
    phase = jnp.zeros((size, size), jnp.int32)
    for p in range(1, phases):
        phase = phase + jnp.where(ordered >= p * part, 1, 0)
    hit = natural == phases * (ordered - phase * part) + phase
    return jnp.where(hit, 1.0, 0.0).astype(BF16)


def rounded(x):
    return x.astype(BF16).astype(F32)


def kernel(
    nb, nr,
    fine, mid, top, w2, w3, dw, pw_in, gain, bias,
    out_f, out_m, out_t,
    afine, amid, atop, pw, act, sp, raw_f, raw_d, raw_m, raw_t,
    cpf, cpm, pool_f, pool_m, nf, nm, nt,
    up_f, dn_f, up_m, dn_m, rup_f, rdn_f, rup_m, rdn_m, rup_t, rdn_t,
    perm_f, perm_m, stat_b, stat_r, of_v, om_v, ot_v,
    sb_s, sb_r, sr_s, sr_r, h_s, h_r, loc, outs,
):
    b_me = lax.axis_index("batch")
    r_me = lax.axis_index("rows")
    has_up = r_me > 0
    has_dn = r_me < nr - 1
    above = jnp.maximum(r_me - 1, 0)
    below = jnp.minimum(r_me + 1, nr - 1)
    Rf, Wf, C = fine.shape[1:]
    Rm, Wm = mid.shape[1:3]
    Rt, J = top.shape[1:3]
    Pf, Pm = Wf // J, Wm // J
    images = nb * fine.shape[0]

    loads = [
        pltpu.make_async_copy(mid.at[0], amid.at[pl.ds(2, Rm)], loc.at[0]),
        pltpu.make_async_copy(top.at[0], atop.at[pl.ds(1, Rt)], loc.at[1]),
        pltpu.make_async_copy(pw_in, pw, loc.at[2]),
        pltpu.make_async_copy(fine.at[0], afine.at[pl.ds(1, Rf)], loc.at[3]),
    ]
    for copy in loads:
        copy.start()

    barrier = pltpu.get_barrier_semaphore()
    for d in range(1, nb):
        pl.semaphore_signal(
            barrier, inc=1, device_id={"batch": lax.rem(b_me + d, nb)}, device_id_type=MESH
        )
    for d in range(1, nr):
        pl.semaphore_signal(
            barrier, inc=1, device_id={"rows": lax.rem(r_me + d, nr)}, device_id_type=MESH
        )

    def message(k, src, dst, up):
        return pltpu.make_async_remote_copy(
            src_ref=src, dst_ref=dst, send_sem=h_s.at[k], recv_sem=h_r.at[k],
            device_id={"rows": above if up else below}, device_id_type=MESH,
        )

    def send(k, src, dst, up):
        @pl.when(has_up if up else has_dn)
        def _():
            message(k, src, dst, up).start()

    def arrive(k, src, dst, up):
        @pl.when(has_dn if up else has_up)
        def _():
            message(k, src, dst, up).wait_recv()

        @pl.when(has_up if up else has_dn)
        def _():
            message(k, src, dst, up).wait_send()

    def spread_copies(store, sends, recvs, node, me, count, axis):
        return [
            pltpu.make_async_remote_copy(
                src_ref=store.at[node, me], dst_ref=store.at[node, me],
                send_sem=sends.at[node, d], recv_sem=recvs.at[node, d],
                device_id={axis: lax.rem(me + d, count)}, device_id_type=MESH,
            )
            for d in range(1, count)
        ]

    def stats_begin(node, total, square):
        stat_b[node, b_me, 0:1, :] = total
        stat_b[node, b_me, 1:2, :] = square
        copies = spread_copies(stat_b, sb_s, sb_r, node, b_me, nb, "batch")
        for copy in copies:
            copy.start()
        return copies

    def stats_middle(node, copies):
        for copy in copies:
            copy.wait_recv()
        stat_r[node, r_me] = jnp.sum(stat_b[node], axis=0)
        second = spread_copies(stat_r, sr_s, sr_r, node, r_me, nr, "rows")
        for copy in second:
            copy.start()
        for copy in copies:
            copy.wait_send()
        return second

    def stats_end(node, copies, layer, which, count):
        for copy in copies:
            copy.wait_recv()
        sums = jnp.sum(stat_r[node], axis=0)
        for copy in copies:
            copy.wait_send()
        center = sums[0:1] / count
        spread = sums[1:2] / count - center * center
        scale = lax.rsqrt(spread + 1e-05) * gain[layer, which : which + 1, :]
        return center, scale, bias[layer, which : which + 1, :]

    def normal(x, stats):
        center, scale, shift = stats
        return (x - center) * scale + shift

    def coefficients(weights):
        total = weights[0]
        for w in weights[1:]:
            total = total + w
        inverse = 0.5 / jnp.full((1, C), total + 0.0001, F32)
        return [jnp.full((1, C), w, F32) * inverse for w in weights]

    def activate(row, p, half, valid):
        a = rounded(half + half * jnp.tanh(half))
        act[row, p, pl.ds(PAD, J), :] = jnp.where(valid, a, 0.0)

    def depthwise(layer, which, rows, phases):
        taps = []
        for i in range(3):
            k = dw[layer, which, i].astype(F32)
            taps.append([k[j : j + 1] for j in range(3)])

        def body(r, carry):
            for p in range(phases):
                total = None
                for i in range(3):
                    for j in range(3):
                        q, at = p + j - 1, PAD
                        if q < 0:
                            q, at = phases - 1, PAD - 1
                        elif q >= phases:
                            q, at = 0, PAD + 1
                        term = act[r + i, q, pl.ds(at, J), :] * taps[i][j]
                        total = term if total is None else total + term
                sp[pl.ds(pl.multiple_of((r * phases + p) * J, J), J), :] = total.astype(BF16)
            return carry

        lax.fori_loop(0, rows, body, 0)

    def pointwise(layer, which, rows, phases, chunk, dst, skip):
        width = phases * J

        def one(first, carry):
            y = jnp.dot(
                sp[pl.ds(pl.multiple_of(first * width, J), chunk * width), :],
                pw[layer, which], preferred_element_type=F32,
            )
            for r in range(chunk):
                for p in range(phases):
                    a = (r * phases + p) * J
                    dst[first + r, p, pl.ds(0, J), :] = y[a : a + J]
            kept = y[skip * width : (chunk - skip) * width]
            return (
                carry[0] + jnp.sum(kept, axis=0, keepdims=True),
                carry[1] + jnp.sum(kept * kept, axis=0, keepdims=True),
            )

        zero = jnp.zeros((1, C), F32)
        if chunk == rows:
            return one(0, (zero, zero))
        return lax.fori_loop(0, rows // chunk, lambda i, c: one(i * chunk, c), (zero, zero))

    def column_pool(src, row, q, phases):
        a = jnp.maximum(src[row, 2 * q, pl.ds(0, J), :], src[row, 2 * q + 1, pl.ds(0, J), :])
        if 2 * q + 2 < phases:
            return jnp.maximum(a, src[row, 2 * q + 2, pl.ds(0, J), :])
        return jnp.maximum(a, src[row, 0, pl.ds(1, J), :])

    act[:, :, 0:PAD, :] = jnp.zeros((Rf + 2, Pf, PAD, C), F32)
    act[:, :, J + PAD : J + 2 * PAD, :] = jnp.zeros((Rf + 2, Pf, PAD, C), F32)
    raw_f[:, :, J : J + PAD, :] = jnp.full((Rf, Pf, PAD, C), -jnp.inf, F32)
    raw_m[:, :, J : J + PAD, :] = jnp.full((Rm, Pm, PAD, C), -jnp.inf, F32)

    pl.semaphore_wait(barrier, nb + nr - 2)
    first = [
        (0, mid.at[0, pl.ds(0, 2)], amid.at[pl.ds(Rm + 2, 2)], True),
        (1, mid.at[0, pl.ds(Rm - 2, 2)], amid.at[pl.ds(0, 2)], False),
        (2, top.at[0, 0], atop.at[Rt + 1], True),
        (3, top.at[0, Rt - 1], atop.at[0], False),
        (4, fine.at[0, 0], afine.at[Rf + 1], True),
        (5, fine.at[0, Rf - 1], afine.at[0], False),
    ]
    for m in first:
        send(*m)
    perm_f[0] = permutation(Wf, Pf, False)
    perm_f[1] = permutation(Wf, Pf, True)
    perm_m[0] = permutation(Wm, Pm, False)
    perm_m[1] = permutation(Wm, Pm, True)
    for copy in loads[:2]:
        copy.wait()
    for m in first[:4]:
        arrive(*m)

    def order_mid(e, carry):
        y = jnp.dot(perm_m[0], amid[e], preferred_element_type=F32).astype(BF16)
        for p in range(Pm):
            nm[0, e, p] = y[p * J : (p + 1) * J]
        return carry

    lax.fori_loop(0, Rm + 4, order_mid, 0)
    nt[0] = atop[...]
    loads[2].wait()

    pending = []
    for layer in range(LAYERS):
        last = layer == LAYERS - 1
        base = NODES * layer
        hb = 6 + 12 * layer

        c0 = coefficients([w2[layer, 0, 0], w2[layer, 0, 1]])

        def act0(e, carry):
            valid = ((e >= 2) | has_up) & ((e < Rm + 2) | has_dn)
            coarse = nt[layer, e // 2].astype(F32) * c0[1]
            for p in range(Pm):
                activate(e, p, nm[layer, e, p].astype(F32) * c0[0] + coarse, valid)
            return carry

        lax.fori_loop(0, Rm + 4, act0, 0)
        depthwise(layer, 0, Rm + 2, Pm)
        t, s = pointwise(layer, 0, Rm + 2, Pm, Rm + 2, raw_d, 1)
        copies = stats_begin(base, t, s)
        if layer == 0:
            loads[3].wait()
            for m in first[4:]:
                arrive(*m)

            def order_fine(e, carry):
                y = jnp.dot(perm_f[0], afine[e], preferred_element_type=F32).astype(BF16)
                for p in range(Pf):
                    nf[0, e, p] = y[p * J : (p + 1) * J]
                return carry

            lax.fori_loop(0, Rf + 2, order_fine, 0)
        second = stats_middle(base, copies)
        sd = stats_end(base, second, layer, 0, float(images * nr * Rm * Wm))

        for m in pending:
            arrive(*m)
        pending = []
        c1 = coefficients([w2[layer, 1, 0], w2[layer, 1, 1]])

        def norm_d(e, carry):
            for p in range(Pm):
                raw_d[e, p] = rounded(normal(raw_d[e, p], sd))
            return carry

        lax.fori_loop(0, Rm + 2, norm_d, 0)

        def act1(e, carry):
            valid = ((e >= 1) | has_up) & ((e < Rf + 1) | has_dn)
            for p in range(Pf):
                down = raw_d[(e + 1) // 2, p // 2] * c1[1]
                activate(e, p, nf[layer, e, p].astype(F32) * c1[0] + down, valid)
            return carry

        lax.fori_loop(0, Rf + 2, act1, 0)
        depthwise(layer, 1, Rf, Pf)
        t, s = pointwise(layer, 1, Rf, Pf, 2, raw_f, 0)
        copies = stats_begin(base + 1, t, s)

        def pool_cols_f(r, carry):
            for q in range(Pm):
                cpf[r, q] = column_pool(raw_f, r, q, Pf)
            return carry

        lax.fori_loop(0, Rf, pool_cols_f, 0)
        up_f[0] = cpf[0]
        up_f[1] = jnp.maximum(jnp.maximum(cpf[0], cpf[1]), cpf[2])
        dn_f[...] = jnp.maximum(cpf[Rf - 2], cpf[Rf - 1])
        edge = [
            (hb, up_f, rup_f.at[layer], True),
            (hb + 1, dn_f, rdn_f.at[layer], False),
        ]
        for m in edge:
            send(*m)

        def pool_rows_f(i, carry):
            pool_f[i + 1] = jnp.maximum(
                jnp.maximum(cpf[2 * i], cpf[2 * i + 1]), cpf[2 * i + 2]
            )
            return carry

        lax.fori_loop(0, Rm - 1, pool_rows_f, 0)
        second = stats_middle(base + 1, copies)
        for m in edge:
            arrive(*m)
        pool_f[0] = jnp.maximum(rdn_f[layer], cpf[0])
        pool_f[Rm] = jnp.maximum(dn_f[...], jnp.where(has_dn, rup_f[layer, 0], -jnp.inf))
        pool_f[Rm + 1] = rup_f[layer, 1]
        sf = stats_end(base + 1, second, layer, 1, float(images * nr * Rf * Wf))

        c2 = coefficients([w3[layer, 0], w3[layer, 1], w3[layer, 2]])

        def act2(e, carry):
            valid = ((e >= 1) | has_up) & ((e < Rm + 1) | has_dn)
            for p in range(Pm):
                half = nm[layer, e + 1, p].astype(F32) * c2[0] + raw_d[e, p] * c2[1]
                half = half + rounded(normal(pool_f[e, p], sf)) * c2[2]
                activate(e, p, half, valid)
            return carry

        lax.fori_loop(0, Rm + 2, act2, 0)
        depthwise(layer, 2, Rm, Pm)
        t, s = pointwise(layer, 2, Rm, Pm, Rm, raw_m, 0)
        copies = stats_begin(base + 2, t, s)

        def pool_cols_m(r, carry):
            cpm[r] = column_pool(raw_m, r, 0, Pm)
            return carry

        lax.fori_loop(0, Rm, pool_cols_m, 0)
        up_m[0] = cpm[0]
        up_m[1] = jnp.maximum(jnp.maximum(cpm[0], cpm[1]), cpm[2])
        dn_m[...] = jnp.maximum(cpm[Rm - 2], cpm[Rm - 1])
        edge = [
            (hb + 2, up_m, rup_m.at[layer], True),
            (hb + 3, dn_m, rdn_m.at[layer], False),
        ]
        for m in edge:
            send(*m)

        def pool_rows_m(i, carry):
            pool_m[i + 1] = jnp.maximum(
                jnp.maximum(cpm[2 * i], cpm[2 * i + 1]), cpm[2 * i + 2]
            )
            return carry

        lax.fori_loop(0, Rt - 1, pool_rows_m, 0)

        if last:

            def finish_f(r, carry):
                for p in range(Pf):
                    sp[pl.ds(p * J, J), :] = normal(raw_f[r, p, pl.ds(0, J), :], sf).astype(BF16)
                of_v[r] = jnp.dot(
                    perm_f[1], sp[pl.ds(0, Wf), :], preferred_element_type=F32
                ).astype(BF16)
                return carry

            lax.fori_loop(0, Rf, finish_f, 0)
            copy_f = pltpu.make_async_copy(of_v, out_f.at[0], outs.at[0])
            copy_f.start()
        else:

            def finish_f(r, carry):
                for p in range(Pf):
                    nf[layer + 1, r + 1, p] = normal(
                        raw_f[r, p, pl.ds(0, J), :], sf
                    ).astype(BF16)
                return carry

            lax.fori_loop(0, Rf, finish_f, 0)
            pending += [
                (hb + 4, nf.at[layer + 1, 1], nf.at[layer + 1, Rf + 1], True),
                (hb + 5, nf.at[layer + 1, Rf], nf.at[layer + 1, 0], False),
            ]
        second = stats_middle(base + 2, copies)
        for m in edge:
            arrive(*m)
        pool_m[0] = jnp.maximum(rdn_m[layer], cpm[0])
        pool_m[Rt] = jnp.maximum(dn_m[...], jnp.where(has_dn, rup_m[layer, 0], -jnp.inf))
        pool_m[Rt + 1] = rup_m[layer, 1]
        sm = stats_end(base + 2, second, layer, 2, float(images * nr * Rm * Wm))

        c3 = coefficients([w2[layer, 2, 0], w2[layer, 2, 1]])

        def act3(e, carry):
            valid = ((e >= 1) | has_up) & ((e < Rt + 1) | has_dn)
            half = nt[layer, e].astype(F32) * c3[0]
            half = half + rounded(normal(pool_m[e], sm)) * c3[1]
            activate(e, 0, half, valid)
            return carry

        lax.fori_loop(0, Rt + 2, act3, 0)
        depthwise(layer, 3, Rt, 1)
        t, s = pointwise(layer, 3, Rt, 1, Rt, raw_t, 0)
        copies = stats_begin(base + 3, t, s)
        if last:

            def finish_m(r, carry):
                for p in range(Pm):
                    sp[pl.ds(p * J, J), :] = normal(raw_m[r, p, pl.ds(0, J), :], sm).astype(BF16)
                om_v[r] = jnp.dot(
                    perm_m[1], sp[pl.ds(0, Wm), :], preferred_element_type=F32
                ).astype(BF16)
                return carry

            lax.fori_loop(0, Rm, finish_m, 0)
            copy_m = pltpu.make_async_copy(om_v, out_m.at[0], outs.at[1])
            copy_m.start()
            second = stats_middle(base + 3, copies)
            st = stats_end(base + 3, second, layer, 3, float(images * nr * Rt * J))
            for r in range(Rt):
                ot_v[r] = normal(raw_t[r, 0], st).astype(BF16)
            copy_t = pltpu.make_async_copy(ot_v, out_t.at[0], outs.at[2])
            copy_t.start()
            for copy in (copy_f, copy_m, copy_t):
                copy.wait()
        else:
            edge = [
                (hb + 6, raw_t.at[0, 0], rup_t.at[layer], True),
                (hb + 7, raw_t.at[Rt - 1, 0], rdn_t.at[layer], False),
            ]
            for m in edge:
                send(*m)

            def finish_m(r, carry):
                for p in range(Pm):
                    nm[layer + 1, r + 2, p] = normal(
                        raw_m[r, p, pl.ds(0, J), :], sm
                    ).astype(BF16)
                return carry

            lax.fori_loop(0, Rm, finish_m, 0)
            rows = [
                (hb + 8, nm.at[layer + 1, pl.ds(2, 2)], nm.at[layer + 1, pl.ds(Rm + 2, 2)], True),
                (hb + 9, nm.at[layer + 1, pl.ds(Rm, 2)], nm.at[layer + 1, pl.ds(0, 2)], False),
            ]
            for m in rows:
                send(*m)
            for m in pending:
                send(*m)
            second = stats_middle(base + 3, copies)
            for m in edge + rows:
                arrive(*m)
            st = stats_end(base + 3, second, layer, 3, float(images * nr * Rt * J))
            nt[layer + 1, 0] = normal(rdn_t[layer], st).astype(BF16)
            for r in range(Rt):
                nt[layer + 1, r + 1] = normal(raw_t[r, 0], st).astype(BF16)
            nt[layer + 1, Rt + 1] = normal(rup_t[layer], st).astype(BF16)


def body(nb, nr, fine, mid, top, w2, w3, dw, pw, gain, bias):
    _, Rf, Wf, C = fine.shape
    _, Rm, Wm, _ = mid.shape
    _, Rt, J, _ = top.shape
    Pf, Pm = Wf // J, Wm // J
    assert fine.shape[0] == 1 and Pf == 4 and Pm == 2 and J % 16 == 0
    assert Rf == 2 * Rm and Rm == 2 * Rt and Rt >= 2
    L = LAYERS
    V = pltpu.VMEM
    scratch = [
        V((Rf + 2, Wf, C), BF16), V((Rm + 4, Wm, C), BF16), V((Rt + 2, J, C), BF16),
        V(pw.shape, BF16),
        V((Rf + 2, Pf, J + 2 * PAD, C), F32), V((Rf * Wf, C), BF16),
        V((Rf, Pf, J + PAD, C), F32), V((Rm + 2, Pm, J, C), F32),
        V((Rm, Pm, J + PAD, C), F32), V((Rt, 1, J, C), F32),
        V((Rf, Pm, J, C), F32), V((Rm, J, C), F32),
        V((Rm + 2, Pm, J, C), F32), V((Rt + 2, J, C), F32),
        V((L, Rf + 2, Pf, J, C), BF16), V((L, Rm + 4, Pm, J, C), BF16), V((L, Rt + 2, J, C), BF16),
        V((2, Pm, J, C), F32), V((Pm, J, C), F32), V((2, J, C), F32), V((J, C), F32),
        V((L, 2, Pm, J, C), F32), V((L, Pm, J, C), F32),
        V((L, 2, J, C), F32), V((L, J, C), F32),
        V((L, J, C), F32), V((L, J, C), F32),
        V((2, Wf, Wf), BF16), V((2, Wm, Wm), BF16),
        V((L * NODES, nb, 2, C), F32), V((L * NODES, nr, 2, C), F32),
        V((Rf, Wf, C), BF16), V((Rm, Wm, C), BF16), V((Rt, J, C), BF16),
        pltpu.SemaphoreType.DMA((L * NODES, nb)), pltpu.SemaphoreType.DMA((L * NODES, nb)),
        pltpu.SemaphoreType.DMA((L * NODES, nr)), pltpu.SemaphoreType.DMA((L * NODES, nr)),
        pltpu.SemaphoreType.DMA((6 + 12 * L,)), pltpu.SemaphoreType.DMA((6 + 12 * L,)),
        pltpu.SemaphoreType.DMA((4,)), pltpu.SemaphoreType.DMA((3,)),
    ]
    hbm = pl.BlockSpec(memory_space=pl.ANY)
    vmem = pl.BlockSpec(memory_space=pltpu.VMEM)
    smem = pl.BlockSpec(memory_space=pltpu.SMEM)
    return tuple(pl.pallas_call(
        functools.partial(kernel, nb, nr),
        out_shape=[jax.ShapeDtypeStruct(a.shape, BF16) for a in (fine, mid, top)],
        in_specs=[hbm, hbm, hbm, smem, smem, vmem, hbm, vmem, vmem],
        out_specs=[hbm, hbm, hbm],
        scratch_shapes=scratch,
        name="bifpn",
        compiler_params=pltpu.CompilerParams(
            collective_id=0, has_side_effects=True, vmem_limit_bytes=56 * 2**20
        ),
    )(fine, mid, top, w2, w3, dw, pw, gain, bias))


def solution(mesh):
    level = P("batch", "rows", None, None)
    return jax.shard_map(
        functools.partial(body, mesh.shape["batch"], mesh.shape["rows"]),
        mesh=mesh,
        in_specs=(level,) * 3 + (P(),) * 6,
        out_specs=(level,) * 3,
        check_vma=False,
    )
```

```python
import functools

import jax
import jax.numpy as jnp
from jax import lax
from jax.experimental import pallas as pl
from jax.experimental.pallas import tpu as pltpu
from jax.sharding import PartitionSpec as P

LAYERS = 2
NODES = 4
MESH = pl.DeviceIdType.MESH
F32 = jnp.float32
BF16 = jnp.bfloat16
PAD = 8


def permutation(size, phases, inverse):
    part = size // phases
    natural = lax.broadcasted_iota(jnp.int32, (size, size), 0 if inverse else 1)
    ordered = lax.broadcasted_iota(jnp.int32, (size, size), 1 if inverse else 0)
    phase = jnp.zeros((size, size), jnp.int32)
    for p in range(1, phases):
        phase = phase + jnp.where(ordered >= p * part, 1, 0)
    hit = natural == phases * (ordered - phase * part) + phase
    return jnp.where(hit, 1.0, 0.0).astype(BF16)


def rounded(x):
    return x.astype(BF16).astype(F32)


def kernel(
    nb, nr,
    fine, mid, top, w2, w3, dw, pw_in, gain, bias,
    out_f, out_m, out_t,
    afine, amid, atop, pw, act, sp, raw_f, raw_d, raw_m, raw_t,
    cpf, cpm, pool_f, pool_m, nf, nm, nt,
    up_f, dn_f, up_m, dn_m, rup_f, rdn_f, rup_m, rdn_m, rup_t, rdn_t, edge_t,
    perm_f, perm_m, stat_b,
    sb_s, sb_r, h_s, h_r, loc,
):
    b_me = lax.axis_index("batch")
    r_me = lax.axis_index("rows")
    has_up = r_me > 0
    has_dn = r_me < nr - 1
    above = jnp.maximum(r_me - 1, 0)
    below = jnp.minimum(r_me + 1, nr - 1)
    Rf, Wf, C = fine.shape[1:]
    Rm, Wm = mid.shape[1:3]
    Rt, J = top.shape[1:3]
    Pf, Pm = Wf // J, Wm // J
    images = nb * fine.shape[0]

    loads = [
        pltpu.make_async_copy(mid.at[0], amid.at[pl.ds(2, Rm)], loc.at[0]),
        pltpu.make_async_copy(top.at[0], atop.at[pl.ds(1, Rt)], loc.at[1]),
        pltpu.make_async_copy(pw_in, pw, loc.at[2]),
        pltpu.make_async_copy(fine.at[0], afine.at[pl.ds(1, Rf)], loc.at[3]),
    ]
    for copy in loads:
        copy.start()

    barrier = pltpu.get_barrier_semaphore()
    for d in range(1, nb * nr):
        pl.semaphore_signal(
            barrier, inc=1,
            device_id={"batch": lax.rem(b_me + d // nr, nb), "rows": lax.rem(r_me + d % nr, nr)},
            device_id_type=MESH,
        )

    def message(k, src, dst, up):
        return pltpu.make_async_remote_copy(
            src_ref=src, dst_ref=dst, send_sem=h_s.at[k], recv_sem=h_r.at[k],
            device_id={"rows": above if up else below}, device_id_type=MESH,
        )

    def send(k, src, dst, up):
        @pl.when(has_up if up else has_dn)
        def _():
            message(k, src, dst, up).start()

    def arrive(k, src, dst, up):
        @pl.when(has_dn if up else has_up)
        def _():
            message(k, src, dst, up).wait_recv()

        @pl.when(has_up if up else has_dn)
        def _():
            message(k, src, dst, up).wait_send()

    def stats_begin(node, total, square):
        me = b_me * nr + r_me
        stat_b[node, me, 0:1, :] = total
        stat_b[node, me, 1:2, :] = square
        copies = []
        for db in range(nb):
            for dr in range(nr):
                d = db * nr + dr
                if d:
                    copies.append(pltpu.make_async_remote_copy(
                        src_ref=stat_b.at[node, me], dst_ref=stat_b.at[node, me],
                        send_sem=sb_s.at[d], recv_sem=sb_r.at[node, d],
                        device_id={"batch": lax.rem(b_me + db, nb), "rows": lax.rem(r_me + dr, nr)},
                        device_id_type=MESH,
                    ))
                    copies[-1].start()
        return copies

    def stats_end(node, copies, layer, which, count):
        for copy in copies:
            copy.wait_recv()
        sums = jnp.sum(stat_b[node], axis=0)
        for copy in copies:
            copy.wait_send()
        center = sums[0:1] / count
        spread = sums[1:2] / count - center * center
        scale = lax.rsqrt(spread + 1e-05) * gain[layer, which : which + 1, :]
        return center, scale, bias[layer, which : which + 1, :]

    def normal(x, stats):
        center, scale, shift = stats
        return (x - center) * scale + shift

    def coefficients(weights):
        total = weights[0]
        for w in weights[1:]:
            total = total + w
        inverse = 0.5 / jnp.full((1, C), total + 0.0001, F32)
        return [jnp.full((1, C), w, F32) * inverse for w in weights]

    def activate(row, p, half, valid):
        a = rounded(half + half * jnp.tanh(half))
        act[row, p, pl.ds(PAD, J), :] = jnp.where(valid, a, 0.0)

    def depthwise(layer, which, rows, phases, body_only=False):
        taps = []
        for i in range(3):
            rows_of = [dw[layer, i, j].astype(F32) for j in range(3)]
            taps.append([k[which : which + 1] for k in rows_of])

        def body(r, carry):
            for p in range(phases):
                total = None
                for i in range(3):
                    for j in range(3):
                        q, at = p + j - 1, PAD
                        if q < 0:
                            q, at = phases - 1, PAD - 1
                        elif q >= phases:
                            q, at = 0, PAD + 1
                        term = act[r + i, q, pl.ds(at, J), :] * taps[i][j]
                        total = term if total is None else total + term
                sp[pl.ds(pl.multiple_of((r * phases + p) * J, J), J), :] = total.astype(BF16)
            return carry

        if body_only:
            return body
        lax.fori_loop(0, rows, body, 0)

    def fused(layer, which, rows, phases, chunk, dst):
        one_row = depthwise(layer, which, rows, phases, True)
        product = pointwise(layer, which, rows, phases, chunk, dst, 0, True)
        zero = jnp.zeros((1, C), F32)
        for r in range(chunk):
            one_row(r, 0)

        def step(i, carry):
            carry = product(i * chunk, carry)
            for r in range(chunk):
                one_row((i + 1) * chunk + r, 0)
            return carry

        carry = lax.fori_loop(0, rows // chunk - 1, step, (zero, zero))
        return product(rows - chunk, carry)

    def pointwise(layer, which, rows, phases, chunk, dst, skip, body_only=False):
        width = phases * J

        def one(first, carry):
            y = jnp.dot(
                sp[pl.ds(pl.multiple_of(first * width, J), chunk * width), :],
                pw[layer, which], preferred_element_type=F32,
            )
            for r in range(chunk):
                for p in range(phases):
                    a = (r * phases + p) * J
                    dst[first + r, p, pl.ds(0, J), :] = y[a : a + J]
            kept = y[skip * width : (chunk - skip) * width]
            return (
                carry[0] + jnp.sum(kept, axis=0, keepdims=True),
                carry[1] + jnp.sum(kept * kept, axis=0, keepdims=True),
            )

        if body_only:
            return one
        zero = jnp.zeros((1, C), F32)
        if chunk == rows:
            return one(0, (zero, zero))
        return lax.fori_loop(0, rows // chunk, lambda i, c: one(i * chunk, c), (zero, zero))

    def column_pool(src, row, q, phases):
        a = jnp.maximum(src[row, 2 * q, pl.ds(0, J), :], src[row, 2 * q + 1, pl.ds(0, J), :])
        if 2 * q + 2 < phases:
            return jnp.maximum(a, src[row, 2 * q + 2, pl.ds(0, J), :])
        return jnp.maximum(a, src[row, 0, pl.ds(1, J), :])

    act[:, :, 0:PAD, :] = jnp.zeros((Rf + 2, Pf, PAD, C), F32)
    act[:, :, J + PAD : J + 2 * PAD, :] = jnp.zeros((Rf + 2, Pf, PAD, C), F32)
    raw_f[:, :, J : J + PAD, :] = jnp.full((Rf, Pf, PAD, C), -jnp.inf, F32)
    raw_m[:, :, J : J + PAD, :] = jnp.full((Rm, Pm, PAD, C), -jnp.inf, F32)

    pl.semaphore_wait(barrier, nb * nr - 1)
    first = [
        (0, mid.at[0, pl.ds(0, 2)], amid.at[pl.ds(Rm + 2, 2)], True),
        (1, mid.at[0, pl.ds(Rm - 2, 2)], amid.at[pl.ds(0, 2)], False),
        (2, top.at[0, 0], atop.at[Rt + 1], True),
        (3, top.at[0, Rt - 1], atop.at[0], False),
        (4, fine.at[0, 0], afine.at[Rf + 1], True),
        (5, fine.at[0, Rf - 1], afine.at[0], False),
    ]
    for m in first:
        send(*m)
    perm_f[0] = permutation(Wf, Pf, False)
    perm_f[1] = permutation(Wf, Pf, True)
    perm_m[0] = permutation(Wm, Pm, False)
    perm_m[1] = permutation(Wm, Pm, True)
    for copy in loads[:2]:
        copy.wait()
    for m in first[:4]:
        arrive(*m)

    def order_mid(e, carry):
        y = jnp.dot(perm_m[0], amid[e], preferred_element_type=F32).astype(BF16)
        for p in range(Pm):
            nm[0, e, p] = y[p * J : (p + 1) * J]
        return carry

    lax.fori_loop(0, Rm + 4, order_mid, 0)
    nt[0] = atop[...]
    loads[2].wait()

    pending = []
    for layer in range(LAYERS):
        last = layer == LAYERS - 1
        base = NODES * layer
        hb = 6 + 12 * layer

        c0 = coefficients([w2[layer, 0, 0], w2[layer, 1, 0]])

        def act0(e, carry):
            valid = ((e >= 2) | has_up) & ((e < Rm + 2) | has_dn)
            coarse = nt[layer, e // 2].astype(F32) * c0[1]
            for p in range(Pm):
                activate(e, p, nm[layer, e, p].astype(F32) * c0[0] + coarse, valid)
            return carry

        lax.fori_loop(0, Rm + 4, act0, 0)
        depthwise(layer, 0, Rm + 2, Pm)
        t, s = pointwise(layer, 0, Rm + 2, Pm, Rm + 2, raw_d, 1)
        copies = stats_begin(base, t, s)
        if layer == 0:
            loads[3].wait()
            for m in first[4:]:
                arrive(*m)

            def order_fine(e, carry):
                y = jnp.dot(perm_f[0], afine[e], preferred_element_type=F32).astype(BF16)
                for p in range(Pf):
                    nf[0, e, p] = y[p * J : (p + 1) * J]
                return carry

            lax.fori_loop(0, Rf + 2, order_fine, 0)
        sd = stats_end(base, copies, layer, 0, float(images * nr * Rm * Wm))

        for m in pending:
            arrive(*m)
        pending = []
        c1 = coefficients([w2[layer, 0, 1], w2[layer, 1, 1]])

        def norm_d(e, carry):
            for p in range(Pm):
                raw_d[e, p] = rounded(normal(raw_d[e, p], sd))
            return carry

        lax.fori_loop(0, Rm + 2, norm_d, 0)

        def act1(e, carry):
            valid = ((e >= 1) | has_up) & ((e < Rf + 1) | has_dn)
            for p in range(Pf):
                down = raw_d[(e + 1) // 2, p // 2] * c1[1]
                activate(e, p, nf[layer, e, p].astype(F32) * c1[0] + down, valid)
            return carry

        lax.fori_loop(0, Rf + 2, act1, 0)
        t, s = fused(layer, 1, Rf, Pf, 2, raw_f)
        copies = stats_begin(base + 1, t, s)

        def pool_cols_f(r, carry):
            for q in range(Pm):
                cpf[r, q] = column_pool(raw_f, r, q, Pf)
            return carry

        lax.fori_loop(0, Rf, pool_cols_f, 0)
        up_f[0] = cpf[0].astype(BF16)
        up_f[1] = jnp.maximum(jnp.maximum(cpf[0], cpf[1]), cpf[2]).astype(BF16)
        bottom = jnp.maximum(cpf[Rf - 2], cpf[Rf - 1])
        dn_f[...] = bottom.astype(BF16)
        pool_f[Rm] = bottom
        edge = [
            (hb, up_f, rup_f.at[layer], True),
            (hb + 1, dn_f, rdn_f.at[layer], False),
        ]
        for m in edge:
            send(*m)

        def pool_rows_f(i, carry):
            pool_f[i + 1] = jnp.maximum(
                jnp.maximum(cpf[2 * i], cpf[2 * i + 1]), cpf[2 * i + 2]
            )
            return carry

        lax.fori_loop(0, Rm - 1, pool_rows_f, 0)
        for m in edge:
            arrive(*m)
        pool_f[0] = jnp.maximum(rdn_f[layer].astype(F32), cpf[0])
        pool_f[Rm] = jnp.maximum(
            pool_f[Rm], jnp.where(has_dn, rup_f[layer, 0].astype(F32), -jnp.inf)
        )
        pool_f[Rm + 1] = rup_f[layer, 1].astype(F32)
        sf = stats_end(base + 1, copies, layer, 1, float(images * nr * Rf * Wf))

        c2 = coefficients([w3[layer, 0], w3[layer, 1], w3[layer, 2]])

        def act2(e, carry):
            valid = ((e >= 1) | has_up) & ((e < Rm + 1) | has_dn)
            for p in range(Pm):
                half = nm[layer, e + 1, p].astype(F32) * c2[0] + raw_d[e, p] * c2[1]
                half = half + rounded(normal(pool_f[e, p], sf)) * c2[2]
                activate(e, p, half, valid)
            return carry

        lax.fori_loop(0, Rm + 2, act2, 0)
        depthwise(layer, 2, Rm, Pm)
        t, s = pointwise(layer, 2, Rm, Pm, Rm, raw_m, 0)
        copies = stats_begin(base + 2, t, s)

        def pool_cols_m(r, carry):
            cpm[r] = column_pool(raw_m, r, 0, Pm)
            return carry

        lax.fori_loop(0, Rm, pool_cols_m, 0)
        up_m[0] = cpm[0].astype(BF16)
        up_m[1] = jnp.maximum(jnp.maximum(cpm[0], cpm[1]), cpm[2]).astype(BF16)
        bottom = jnp.maximum(cpm[Rm - 2], cpm[Rm - 1])
        dn_m[...] = bottom.astype(BF16)
        pool_m[Rt] = bottom
        edge = [
            (hb + 2, up_m, rup_m.at[layer], True),
            (hb + 3, dn_m, rdn_m.at[layer], False),
        ]
        for m in edge:
            send(*m)

        def pool_rows_m(i, carry):
            pool_m[i + 1] = jnp.maximum(
                jnp.maximum(cpm[2 * i], cpm[2 * i + 1]), cpm[2 * i + 2]
            )
            return carry

        lax.fori_loop(0, Rt - 1, pool_rows_m, 0)

        if last:

            def finish_f(r, carry):
                for p in range(Pf):
                    sp[pl.ds(p * J, J), :] = normal(raw_f[r, p, pl.ds(0, J), :], sf).astype(BF16)
                out_f[0, r] = jnp.dot(
                    perm_f[1], sp[pl.ds(0, Wf), :], preferred_element_type=F32
                ).astype(BF16)
                return carry

            lax.fori_loop(0, Rf, finish_f, 0)
        else:

            def finish_f(r, carry):
                for p in range(Pf):
                    nf[layer + 1, r + 1, p] = normal(
                        raw_f[r, p, pl.ds(0, J), :], sf
                    ).astype(BF16)
                return carry

            lax.fori_loop(0, Rf, finish_f, 0)
            pending += [
                (hb + 4, nf.at[layer + 1, 1], nf.at[layer + 1, Rf + 1], True),
                (hb + 5, nf.at[layer + 1, Rf], nf.at[layer + 1, 0], False),
            ]
        for m in edge:
            arrive(*m)
        pool_m[0] = jnp.maximum(rdn_m[layer].astype(F32), cpm[0])
        pool_m[Rt] = jnp.maximum(
            pool_m[Rt], jnp.where(has_dn, rup_m[layer, 0].astype(F32), -jnp.inf)
        )
        pool_m[Rt + 1] = rup_m[layer, 1].astype(F32)
        sm = stats_end(base + 2, copies, layer, 2, float(images * nr * Rm * Wm))

        c3 = coefficients([w2[layer, 0, 2], w2[layer, 1, 2]])

        def act3(e, carry):
            valid = ((e >= 1) | has_up) & ((e < Rt + 1) | has_dn)
            half = nt[layer, e].astype(F32) * c3[0]
            half = half + rounded(normal(pool_m[e], sm)) * c3[1]
            activate(e, 0, half, valid)
            return carry

        lax.fori_loop(0, Rt + 2, act3, 0)
        depthwise(layer, 3, Rt, 1)
        t, s = pointwise(layer, 3, Rt, 1, Rt, raw_t, 0)
        copies = stats_begin(base + 3, t, s)
        if last:

            def finish_m(r, carry):
                for p in range(Pm):
                    sp[pl.ds(p * J, J), :] = normal(raw_m[r, p, pl.ds(0, J), :], sm).astype(BF16)
                out_m[0, r] = jnp.dot(
                    perm_m[1], sp[pl.ds(0, Wm), :], preferred_element_type=F32
                ).astype(BF16)
                return carry

            lax.fori_loop(0, Rm, finish_m, 0)
            st = stats_end(base + 3, copies, layer, 3, float(images * nr * Rt * J))
            for r in range(Rt):
                out_t[0, r] = normal(raw_t[r, 0], st).astype(BF16)
        else:
            edge_t[0] = raw_t[0, 0].astype(BF16)
            edge_t[1] = raw_t[Rt - 1, 0].astype(BF16)
            edge = [
                (hb + 6, edge_t.at[0], rup_t.at[layer], True),
                (hb + 7, edge_t.at[1], rdn_t.at[layer], False),
            ]
            for m in edge:
                send(*m)

            def finish_m(r, carry):
                for p in range(Pm):
                    nm[layer + 1, r + 2, p] = normal(
                        raw_m[r, p, pl.ds(0, J), :], sm
                    ).astype(BF16)
                return carry

            lax.fori_loop(0, Rm, finish_m, 0)
            rows = [
                (hb + 8, nm.at[layer + 1, pl.ds(2, 2)], nm.at[layer + 1, pl.ds(Rm + 2, 2)], True),
                (hb + 9, nm.at[layer + 1, pl.ds(Rm, 2)], nm.at[layer + 1, pl.ds(0, 2)], False),
            ]
            for m in rows:
                send(*m)
            for m in pending:
                send(*m)
            for m in edge + rows:
                arrive(*m)
            st = stats_end(base + 3, copies, layer, 3, float(images * nr * Rt * J))
            nt[layer + 1, 0] = normal(rdn_t[layer].astype(F32), st).astype(BF16)
            for r in range(Rt):
                nt[layer + 1, r + 1] = normal(raw_t[r, 0], st).astype(BF16)
            nt[layer + 1, Rt + 1] = normal(rup_t[layer].astype(F32), st).astype(BF16)


def body(nb, nr, fine, mid, top, w2, w3, dw, pw, gain, bias):
    _, Rf, Wf, C = fine.shape
    _, Rm, Wm, _ = mid.shape
    _, Rt, J, _ = top.shape
    Pf, Pm = Wf // J, Wm // J
    assert fine.shape[0] == 1 and Pf == 4 and Pm == 2 and J % 16 == 0
    assert Rf == 2 * Rm and Rm == 2 * Rt and Rt >= 2
    L = LAYERS
    V = pltpu.VMEM
    scratch = [
        V((Rf + 2, Wf, C), BF16), V((Rm + 4, Wm, C), BF16), V((Rt + 2, J, C), BF16),
        V(pw.shape, BF16),
        V((Rf + 2, Pf, J + 2 * PAD, C), F32), V((Rf * Wf, C), BF16),
        V((Rf, Pf, J + PAD, C), F32), V((Rm + 2, Pm, J, C), F32),
        V((Rm, Pm, J + PAD, C), F32), V((Rt, 1, J, C), F32),
        V((Rf, Pm, J, C), F32), V((Rm, J, C), F32),
        V((Rm + 2, Pm, J, C), F32), V((Rt + 2, J, C), F32),
        V((L, Rf + 2, Pf, J, C), BF16), V((L, Rm + 4, Pm, J, C), BF16), V((L, Rt + 2, J, C), BF16),
        V((2, Pm, J, C), BF16), V((Pm, J, C), BF16), V((2, J, C), BF16), V((J, C), BF16),
        V((L, 2, Pm, J, C), BF16), V((L, Pm, J, C), BF16),
        V((L, 2, J, C), BF16), V((L, J, C), BF16),
        V((L, J, C), BF16), V((L, J, C), BF16), V((2, J, C), BF16),
        V((2, Wf, Wf), BF16), V((2, Wm, Wm), BF16),
        V((L * NODES, nb * nr, 2, C), F32),
        pltpu.SemaphoreType.DMA((nb * nr,)), pltpu.SemaphoreType.DMA((L * NODES, nb * nr)),
        pltpu.SemaphoreType.DMA((6 + 12 * L,)), pltpu.SemaphoreType.DMA((6 + 12 * L,)),
        pltpu.SemaphoreType.DMA((4,)),
    ]
    hbm = pl.BlockSpec(memory_space=pl.ANY)
    vmem = pl.BlockSpec(memory_space=pltpu.VMEM)
    smem = pl.BlockSpec(memory_space=pltpu.SMEM)
    return tuple(pl.pallas_call(
        functools.partial(kernel, nb, nr),
        out_shape=[pltpu.VMEM(a.shape, BF16) for a in (fine, mid, top)],
        in_specs=[hbm, hbm, hbm, smem, smem, vmem, hbm, vmem, vmem],
        out_specs=[vmem, vmem, vmem],
        scratch_shapes=scratch,
        name="bifpn",
        compiler_params=pltpu.CompilerParams(
            collective_id=0, has_side_effects=True, vmem_limit_bytes=56 * 2**20
        ),
    )(fine, mid, top, jnp.swapaxes(w2, 1, 2), w3, jnp.transpose(dw, (0, 2, 3, 1, 4)), pw, gain, bias))


def solution(mesh):
    level = P("batch", "rows", None, None)
    return jax.shard_map(
        functools.partial(body, mesh.shape["batch"], mesh.shape["rows"]),
        mesh=mesh,
        in_specs=(level,) * 3 + (P(),) * 6,
        out_specs=(level,) * 3,
        check_vma=False,
    )
```
